128 devices in a mesh: lat: 16 (over x, y_lo, core), lon: 8 (over z, y_hi).
Axes of the slice: x: 4, y: 4 (y_hi: 2, y_lo: 2; y = y_hi * 2 + y_lo), z: 4, core: 2. Of those that a mesh axis runs over, the one named last changes fastest.
Arguments:
- field: bfloat16 [256, 16384], P('lat', 'lon'), may hold values from -6 to 6
- stored_row: int32 [256], replicated, may hold values from 0 to 255, as said below
- row_len: int32 [256], replicated, may hold values from 1537 to 2048
- offset: int32 [256], replicated, may hold values from -2 to 1
- first_weight: bfloat16 [32, 9], replicated, may hold values from -2 to 2
- first_bias: float32 [32], replicated, may hold values from -3 to 3
- second_weight: bfloat16 [64, 288], replicated, may hold values from -0.375 to 0.375
- second_bias: float32 [64], replicated, may hold values from -3 to 3
Outputs:
- pooled: bfloat16 [64, 128, 8192], P(None, 'lat', 'lon')
The draws below stay inside these ranges and needn't reach their ends.
Inputs may be any that keep to these rules, and one draw needn't show every extreme that they name: stored_row is a permutation; the 16 slots of one lat device hold rows of exactly 8 tiles of 16 consecutive rows, 2 rows of each.
All inputs are finite; a program needn't handle non-finite values.
Results may differ from the reference program's by a relative error of at most 0.0031.
The reference program's roundings to bfloat16 on the way (of `ordered`, `regular` and `hidden`) count: a program that leaves them out, or rounds other values in their place, can miss the bound.
Values may be sent and summed in bfloat16 or wider, within the bound.
A program may use at most 128 MiB of HBM per device.

```python
import jax
import jax.numpy as jnp
from jax import lax

RD = 16
Q = 2048
GROUPS = 8
C1 = 32
C2 = 64
D1 = 2
D2 = 8
S = 2048
ROWS = 256
N_LAT = 16
N_LON = 8


def draw_row_len(key, part):
    centre = jax.random.randint(key, (), ROWS // 4, 3 * ROWS // 4 + 1)
    rows_idx = jnp.arange(ROWS, dtype=jnp.int32)
    distance = jnp.abs(rows_idx - centre)
    return (S - distance * (S // 4) // ROWS).astype(jnp.int32)


def draw_stored_row(key, part):
    block_count = ROWS // RD
    capacity = RD // GROUPS
    key_one, key_two, key_three = jax.random.split(key, 3)
    shifts = jax.random.permutation(key_one, block_count)[:GROUPS].astype(jnp.int32)
    slot_perm = jax.vmap(lambda sub_key: jax.random.permutation(sub_key, RD))(jax.random.split(key_two, block_count)).astype(jnp.int32)
    row_perm = jax.vmap(lambda sub_key: jax.random.permutation(sub_key, RD))(jax.random.split(key_three, block_count)).astype(jnp.int32)
    holder = jnp.arange(block_count, dtype=jnp.int32)[:, None]
    within = jnp.broadcast_to(jnp.arange(RD, dtype=jnp.int32)[None, :], (block_count, RD))
    tile_of = (holder + shifts[within // capacity]) % block_count
    target = tile_of * RD + row_perm[tile_of, within]
    slot_index = holder * RD + slot_perm
    return jnp.zeros((ROWS,), jnp.int32).at[slot_index.reshape(-1)].set(target.reshape(-1).astype(jnp.int32))


def with_ends(result, own_key, smallest, largest):
    shape = result.shape
    place = [jax.random.randint(jax.random.fold_in(own_key, axis), (), 0, shape[axis]) for axis in range(len(shape))]
    result = result.at[tuple(place)].set(smallest)
    longest = shape.index(max(shape))
    place[longest] = (place[longest] + 1) % shape[longest]
    return result.at[tuple(place)].set(largest)


def shard_levels(own_key, dims, cuts, least, top_value):
    def one(axis_at, shards_of):
        draws = jax.random.uniform(jax.random.fold_in(jax.random.fold_in(own_key, 6), axis_at), (shards_of,), jnp.float32, least / len(cuts), top_value / len(cuts))
        return jnp.repeat(jnp.exp(draws), dims[axis_at] // shards_of).reshape((-1,) + (1,) * (len(dims) - axis_at - 1))

    factor_of = one(*cuts[0])
    for cut in cuts[1:]:
        factor_of = factor_of * one(*cut)
    return factor_of


def bell_draw(stream_key, dims, width, most, shards=(), kind=jnp.bfloat16):
    result = jax.random.normal(stream_key, dims, jnp.float32) * width
    if len(shards) > 0:
        result = shard_levels(stream_key, dims, shards, -0.22, 0.18) * result
    return jnp.clip(result, min=-most, max=most).astype(kind)


def setup_inputs(seed: int = 0) -> dict:
    seeds = jax.random.split(jax.random.key(seed), 9)
    field = bell_draw(seeds[0], (ROWS, S * N_LON), 1.0, 6.0, ((0, 16), (1, 8)))
    stored_row = draw_stored_row(jax.random.fold_in(seeds[8], 71), 0)
    row_len = draw_row_len(jax.random.fold_in(seeds[8], 71), 0)
    offset = with_ends(jax.random.randint(seeds[3], (ROWS,), -2, 2), jax.random.fold_in(seeds[3], 1), -2, 1).astype(jnp.int32)
    first_weight = bell_draw(seeds[4], (C1, 9), 9 ** -0.5, 2.0)
    first_bias = bell_draw(seeds[5], (C1,), 0.5, 3.0, (), jnp.float32)
    second_weight = bell_draw(seeds[6], (C2, 9 * C1), (9 * C1) ** -0.5, 0.375)
    second_bias = bell_draw(seeds[7], (C2,), 0.5, 3.0, (), jnp.float32)
    return dict(field=field, stored_row=stored_row, row_len=row_len, offset=offset, first_weight=first_weight, first_bias=first_bias, second_weight=second_weight, second_bias=second_bias)


def resample(source, prev_tail, next_head, lengths, offsets, columns):
    index_q = jnp.arange(columns, dtype=jnp.int32)
    length_f = lengths.astype(jnp.float32)[..., None]
    position = (2 * index_q + 1).astype(jnp.float32) * length_f / (2.0 * columns) - 0.5 - 0.25 * offsets.astype(jnp.float32)[..., None]
    floored = jnp.floor(position)
    weight = position - floored
    lower_index = floored.astype(jnp.int32)
    last_slot = source.shape[-1] - 1

    def point_value(index):
        inside = jnp.take_along_axis(source, jnp.clip(index, 0, last_slot), axis=-1).astype(jnp.float32)
        picked = jnp.where(index < 0, prev_tail[..., None].astype(jnp.float32), inside)
        return jnp.where(index >= lengths[..., None], next_head[..., None].astype(jnp.float32), picked)

    return ((1.0 - weight) * point_value(lower_index) + weight * point_value(lower_index + 1)).astype(jnp.bfloat16)


def keep_rows(values, first_row, row_total):
    count_rows = values.shape[-2]
    global_rows = first_row + jnp.arange(count_rows, dtype=jnp.int32)
    kept_mask = (global_rows >= 0) & (global_rows < row_total)
    return jnp.where(kept_mask[:, None], values, jnp.zeros((), values.dtype))


def first_layer(padded, first_weight, first_bias, dilation):
    kernel = first_weight.reshape(first_weight.shape[0], 1, 3, 3)
    summed = lax.conv_general_dilated(padded[None, None], kernel, (1, 1), "VALID", rhs_dilation=(dilation, dilation), dimension_numbers=("NCHW", "OIHW", "NCHW"), preferred_element_type=jnp.float32)[0]
    return jax.nn.gelu(summed + first_bias[:, None, None]).astype(jnp.bfloat16)


def second_layer(hidden, second_weight, second_bias, dilation, out_rows):
    channels = hidden.shape[0]
    outputs = second_weight.shape[0]
    kernel = second_weight.reshape(outputs, 3, 3, channels).transpose(0, 3, 1, 2)
    summed = lax.conv_general_dilated(hidden[None], kernel, (1, 1), "VALID", rhs_dilation=(dilation, dilation), dimension_numbers=("NCHW", "OIHW", "NCHW"), preferred_element_type=jnp.float32)[0]
    active = jax.nn.gelu(summed + second_bias[:, None, None])
    out_cols = active.shape[2]
    return active.reshape(outputs, out_rows // 2, 2, out_cols // 2, 2).mean(axis=(2, 4)).astype(jnp.bfloat16)


def reference(field, stored_row, row_len, offset, first_weight, first_bias, second_weight, second_bias):
    ordered = jnp.zeros_like(field).at[stored_row].set(field)
    source = ordered.reshape(ROWS, N_LON, S)
    lengths = jnp.broadcast_to(row_len[:, None], (ROWS, N_LON))
    offsets = jnp.broadcast_to(offset[:, None], (ROWS, N_LON))
    last_point = jnp.take_along_axis(source, (lengths - 1)[..., None], axis=-1)[..., 0]
    first_point = source[..., 0]
    regular = resample(source, jnp.roll(last_point, 1, axis=1), jnp.roll(first_point, -1, axis=1), lengths, offsets, Q)
    regular = regular.reshape(ROWS, N_LON * Q)
    margin = D1 + D2
    wrapped = jnp.concatenate([regular[:, -margin:], regular, regular[:, :margin]], axis=1)
    padded = jnp.pad(wrapped, ((margin, margin), (0, 0)))

    def one_band(band_index):
        first_row = band_index * RD
        row_piece = lax.dynamic_slice_in_dim(padded, first_row, RD + 2 * margin, axis=0)
        hidden = first_layer(row_piece, first_weight, first_bias, D1)
        hidden = keep_rows(hidden, first_row - D2, ROWS)
        return second_layer(hidden, second_weight, second_bias, D2, RD)

    band_out = lax.map(one_band, jnp.arange(N_LAT, dtype=jnp.int32))
    return band_out.transpose(1, 0, 2, 3).reshape(C2, ROWS // 2, N_LON * Q // 2)
```

```python
import functools
import math

import jax
import jax.numpy as jnp
from jax import lax
from jax.experimental import pallas as pl
from jax.experimental.pallas import tpu as pltpu
from jax.sharding import PartitionSpec as P

Q = 2048
GROUPS = 8
D1 = 2
D2 = 8
F32 = jnp.float32
BF16 = jnp.bfloat16
RE = 40
TILES = 9
WID = TILES * 128
GA = math.sqrt(2.0 / math.pi)
GB = GA * 0.044715


def gelu2(v):
    t = jnp.tanh(v * (v * v * GB + GA))
    return v + v * t


def candidates(u):
    if u == 8:
        return [-1, 0, 12, 13, 14, 15, 16]
    low = math.floor(1.501 * u - 0.008)
    high = 2 * u + 2
    cands = [c for c in range(low, min(high, 15) + 1)]
    if u == 7:
        cands.append(16)
    return cands


def regrid(src, lens, offs, parity, u):
    lane = lax.broadcasted_iota(jnp.int32, (RE, 128), 1)
    m = u * 128 + lane
    if u == 8:
        m = jnp.where(lane >= 64, m - WID, m)
    j = 2 * m + parity
    num = (2 * j + 1) * lens - 2048 - 1024 * offs
    low = num >> 12
    frac = (num & 4095).astype(F32) * (1.0 / 4096.0)
    cands = candidates(u)

    def value(e):
        over = e >= lens
        if 16 in cands:
            past = e - lens
            blk = jnp.where(over, 16, e >> 7)
            idx = jnp.where(over, past, e) & 127
        else:
            blk = e >> 7
            idx = e & 127
        result = None
        for c in cands:
            got = jnp.take_along_axis(src(c), idx, axis=1)
            result = got if result is None else jnp.where(blk == c, got, result)
        return result

    return (1.0 - frac) * value(low) + frac * value(low + 1)


def compute_kernel(t_ref, src_ref, len_ref, off_ref, w1_ref, b1_ref, w2_ref, b2_ref, out_ref, x_ref, band_ref, wide_ref, hid_ref, shift_ref, acc_ref):
    tile = t_ref[0]
    row = lax.broadcasted_iota(jnp.int32, (RE, 128), 0)
    globe = row + tile * 16 - 10
    kept = (globe >= 0) & (globe < 256) & (row < 36)
    lens = len_ref[...]
    offs = off_ref[...]

    lane = lax.broadcasted_iota(jnp.int32, (32, 128), 1)
    taps = w1_ref[...].astype(F32)
    bias = b1_ref[...]
    b_hi = bias.astype(BF16).astype(F32)
    b_mid = (bias - b_hi).astype(BF16).astype(F32)
    b_lo = bias - b_hi - b_mid
    zero = jnp.zeros((32, 128), F32)
    tail = jnp.where(lane == 120, b_hi, jnp.where(lane == 121, b_mid, jnp.where(lane == 122, b_lo, zero)))
    tap_w = [jnp.broadcast_to(taps[:, k : k + 1], (32, 128)) for k in range(9)]
    for p in range(4):
        for q in range(2):
            for a2 in range(4):
                r = 2 * p + q + 8 * a2
                full = tail
                for a in range(3):
                    for b in range(3):
                        full = jnp.where(lane == b * RE + r + 2 * a, tap_w[3 * a + b], full)
                band_ref[pl.ds(((p * 2 + q) * 4 + a2) * 32, 32), :] = full.astype(BF16)

    w2 = w2_ref[...].astype(F32) * 0.5
    gap = jnp.zeros((64, 96), F32)
    wide = jnp.concatenate([jnp.concatenate([w2, gap], axis=1), jnp.concatenate([gap, w2], axis=1)], axis=0)
    k = lax.broadcasted_iota(jnp.int32, (128, 384), 1)
    dead = ((tile == 0) & (k < 96)) | ((tile == 15) & (k >= 288))
    wide_ref[...] = jnp.where(dead, 0.0, wide).astype(BF16)
    b2 = b2_ref[...]

    def src(c):
        return src_ref[:, pl.ds((c + 1) * 128, 128)].astype(F32)

    ones = jnp.ones((8, 128), F32)
    zlane = lax.broadcasted_iota(jnp.int32, (RE, 128), 1)
    for parity in range(2):
        reg = [jnp.where(kept, regrid(src, lens, offs, parity, u), 0.0) for u in range(TILES)]
        for u in range(TILES):
            before, after = reg[u - 1], reg[(u + 1) % TILES]
            left = jnp.where(zlane < 1, pltpu.roll(before, 1, 1), pltpu.roll(reg[u], 1, 1))
            right = jnp.where(zlane >= 127, pltpu.roll(after, 127, 1), pltpu.roll(reg[u], 127, 1))
            x_ref[parity, :, pl.ds(u * 128, 128)] = jnp.concatenate([left, reg[u], right, ones], axis=0).astype(BF16)

    hlane = lax.broadcasted_iota(jnp.int32, (256, 128), 1)

    def step(p, carry):
        band = band_ref[pl.ds(pl.multiple_of(p * 256, 256), 256), :]
        for parity in range(2):
            for u in range(TILES):
                pre = jnp.dot(band, x_ref[parity, :, pl.ds(u * 128, 128)], preferred_element_type=F32)
                hid_ref[parity, :, pl.ds(u * 128, 128)] = gelu2(pre).astype(BF16)
        for parity in range(2):
            for u in range(8):
                mid = hid_ref[parity, :, pl.ds(u * 128, 128)]
                before = hid_ref[parity, :, pl.ds(((u - 1) % TILES) * 128, 128)]
                after = hid_ref[parity, :, pl.ds((u + 1) * 128, 128)]
                left = jnp.concatenate([before[:, 124:], mid[:, :124]], axis=1)
                right = jnp.concatenate([mid[:, 4:], after[:, :4]], axis=1)
                for q in range(2):
                    for a2 in range(4):
                        rows = slice((q * 4 + a2) * 32, (q * 4 + a2 + 1) * 32)
                        for b, part in enumerate((left, mid, right)):
                            shift_ref[parity, pl.ds(q * 384 + (a2 * 3 + b) * 32, 32), pl.ds(u * 128, 128)] = part[rows]
        wide = wide_ref[...]
        for u in range(4):
            cols = pl.ds(u * 256, 256)
            total = None
            for parity in range(2):
                for q in range(2):
                    pre = jnp.dot(wide, shift_ref[parity, pl.ds(q * 384, 384), cols], preferred_element_type=F32)
                    one = gelu2(pre + b2)
                    total = one if total is None else total + one
            total = total * 0.125
            for w in range(2):
                lanes = slice(w * 128, (w + 1) * 128)
                base = (2 * u + w) * 512
                acc_ref[pl.ds(pl.multiple_of(base + p * 64, 64), 64), :] = total[:64, lanes]
                acc_ref[pl.ds(pl.multiple_of(base + p * 64 + 256, 64), 64), :] = total[64:, lanes]
        return carry

    lax.fori_loop(0, 4, step, 0)
    for o in range(64):
        out_ref[o] = jnp.concatenate([acc_ref[pl.ds(u * 512 + o, 8, stride=64), :] for u in range(8)], axis=1).astype(BF16)


def compute(tile, src, lens, offs, w1, b1, w2, b2):
    smem = pl.BlockSpec(memory_space=pltpu.SMEM)
    vmem = pl.BlockSpec(memory_space=pltpu.VMEM)
    return pl.pallas_call(
        compute_kernel,
        out_shape=jax.ShapeDtypeStruct((64, 8, 1024), BF16),
        in_specs=[smem] + [vmem] * 7,
        out_specs=vmem,
        scratch_shapes=[
            pltpu.VMEM((2, 128, WID), BF16),
            pltpu.VMEM((1024, 128), BF16),
            pltpu.VMEM((128, 384), BF16),
            pltpu.VMEM((2, 256, WID), BF16),
            pltpu.VMEM((2, 768, 1024), BF16),
            pltpu.VMEM((4096, 128), F32),
        ],
        compiler_params=pltpu.CompilerParams(vmem_limit_bytes=48 << 20),
    )(tile, src, lens, offs, w1, b1, w2, b2)


def with_halo(block, sides, width):
    for axis, dim in sides:
        count = lax.axis_size(axis)
        forward = [(i, i + 1) for i in range(count - 1)]
        forward.append((count - 1, 0))
        backward = [(target, source) for source, target in forward]
        low = lax.ppermute(
            lax.slice_in_dim(block, block.shape[dim] - width, None, axis=dim), axis, forward
        )
        high = lax.ppermute(lax.slice_in_dim(block, 0, width, axis=dim), axis, backward)
        block = jnp.concatenate([low, block, high], axis=dim)
    return block


def pack_rows(values, stored_row, lat_index, band_count, capacity):
    row_count = values.shape[0]
    held_ids = lax.dynamic_slice_in_dim(stored_row, lat_index * row_count, row_count)
    tile_of = held_ids // row_count
    one_hot = (tile_of[:, None] == jnp.arange(band_count, dtype=jnp.int32)[None, :]).astype(
        jnp.int32
    )
    rank_of = jnp.sum((jnp.cumsum(one_hot, axis=0) - 1) * one_hot, axis=1)
    slot_of = tile_of * capacity + rank_of
    buffer = (
        jnp.zeros((band_count * capacity, values.shape[1]), values.dtype).at[slot_of].set(values)
    )
    return buffer.reshape(band_count, capacity, values.shape[1])


def unpack_rows(arrived, stored_row, lat_index, row_count, band_count, capacity):
    held_all = stored_row.reshape(band_count, row_count)
    tile_of = held_all // row_count
    one_hot = (
        tile_of[:, :, None] == jnp.arange(band_count, dtype=jnp.int32)[None, None, :]
    ).astype(jnp.int32)
    rank_of = jnp.sum((jnp.cumsum(one_hot, axis=1) - 1) * one_hot, axis=2)
    slot_of = jnp.arange(band_count, dtype=jnp.int32)[:, None] * capacity + rank_of
    is_mine = tile_of == lat_index
    target = jnp.where(is_mine, held_all % row_count, row_count)
    source = (
        jnp.zeros((row_count,), jnp.int32)
        .at[target.reshape(-1)]
        .set(slot_of.reshape(-1), mode="drop")
    )
    flat_rows = arrived.reshape(band_count * capacity, arrived.shape[2])
    return jnp.take(flat_rows, source, axis=0)


def per_device(field, stored_row, row_len, offset, first_weight, first_bias, second_weight, second_bias):
    row_count = field.shape[0]
    band_count = lax.axis_size("lat")
    lat_index = lax.axis_index("lat")
    bundle = pack_rows(field, stored_row, lat_index, band_count, row_count // GROUPS)
    arrived = lax.all_to_all(bundle, "lat", split_axis=0, concat_axis=0, tiled=True)
    rows = unpack_rows(arrived, stored_row, lat_index, row_count, band_count, row_count // GROUPS)
    rows = with_halo(rows, (("lat", 0),), D1 + D2)
    ids = jnp.clip(lat_index * row_count - D1 - D2 + jnp.arange(RE, dtype=jnp.int32), 0, 255)
    lens = jnp.take(row_len, ids)
    offs = jnp.take(offset, ids)
    rows = jnp.pad(rows, ((0, RE - rows.shape[0]), (0, 0)))
    tail = jnp.take_along_axis(rows, lens[:, None] - 16 + jnp.arange(16, dtype=jnp.int32)[None, :], axis=1)
    count = lax.axis_size("lon")
    forward = [(i, (i + 1) % count) for i in range(count)]
    backward = [((i + 1) % count, i) for i in range(count)]
    before = lax.ppermute(tail, "lon", forward)
    after = lax.ppermute(rows[:, :16], "lon", backward)
    src = jnp.concatenate([jnp.pad(before, ((0, 0), (112, 0))), rows, jnp.pad(after, ((0, 0), (0, 112)))], axis=1)
    spread = lambda v: jnp.broadcast_to(v[:, None], (RE, 128))
    return compute(
        lat_index[None].astype(jnp.int32),
        src,
        spread(lens),
        spread(offs),
        first_weight,
        first_bias[:, None],
        second_weight,
        jnp.concatenate([second_bias, second_bias])[:, None],
    )


def solution(mesh):
    placed = (P("lat", "lon"), P(), P(), P(), P(), P(), P(), P())
    return jax.shard_map(
        per_device, mesh=mesh, in_specs=placed, out_specs=P(None, "lat", "lon"), check_vma=False
    )
```
